256 devices in a mesh: swap: 16 (over y_hi, z), blk: 16 (over x, y_lo, core).
Axes of the slice: x: 4, y: 4 (y_hi: 2, y_lo: 2; y = y_hi * 2 + y_lo), z: 8, core: 2. Of those that a mesh axis runs over, the one named last changes fastest.
Arguments:
- queries: bfloat16 [32768, 4096], P(('blk', 'swap')), may hold values from -6 to 6
- keys: bfloat16 [32768, 512], P(('blk', 'swap')), may hold values from -6 to 6
- values: bfloat16 [32768, 512], P(('blk', 'swap')), may hold values from -6 to 6
- grad_out: bfloat16 [32768, 4096], P(('blk', 'swap')), may hold values from -6 to 6
- doc_ids: int32 [32768], replicated, may hold values from 0 to 32767, as said below
Outputs:
- grad_queries: bfloat16 [32768, 4096], P(('blk', 'swap'))
- grad_keys: bfloat16 [32768, 512], P(('blk', 'swap'))
- grad_values: bfloat16 [32768, 512], P(('blk', 'swap'))
The draws below stay inside these ranges and needn't reach their ends.
Inputs may be any that keep to these rules, and one draw needn't show every extreme that they name: `doc_ids`: each token's label is the position of the first token of its document, so labels never fall along the sequence; each document holds 1 to 1024 tokens, the last token is a document of its own, and in every draw a document of exactly 1024 tokens ends on the first token of some block of 2048 tokens after the first block.
All inputs are finite; a program needn't handle non-finite values.
Results may differ from the reference program's by a relative error of at most 0.0058.
Values may be sent and summed in bfloat16 or wider, within the bound.
A program may use at most 64 MiB of HBM per device.

```python
import math
import jax
import jax.numpy as jnp
from jax import lax

HEADS = 32
KV_HEADS = 4
HEAD_DIM = 128
MOST = 1024
SEQ_BLK = 2048
SEQ = 32768


def drawn_start(key):
    blocks_total = SEQ // SEQ_BLK
    chosen = jax.random.randint(jax.random.fold_in(key, 11), (), 1, blocks_total)
    return (chosen * SEQ_BLK - MOST + 1).astype(jnp.int32)


def draw_doc_ids(key, part):
    start = drawn_start(key)
    first_factor = jax.random.randint(jax.random.fold_in(key, 21), (SEQ,), 0, MOST)
    second_factor = jax.random.randint(jax.random.fold_in(key, 22), (SEQ,), 0, MOST)
    lengths = 1 + first_factor * second_factor // MOST
    ends = jnp.cumsum(lengths)
    starts = ends - lengths
    places = jnp.arange(SEQ, dtype=jnp.int32)
    flags = jnp.zeros((SEQ,), jnp.int32).at[starts].set(1, mode='drop')
    inside = (places > start) & (places < start + MOST)
    flags = jnp.where(inside, 0, flags)
    flags = jnp.where((places == start) | (places == start + MOST) | (places == 0) | (places == SEQ - 1), 1, flags)
    labels = jnp.where(flags == 1, places, 0)
    return lax.cummax(labels, axis=0).astype(jnp.int32)


def draw_queries(key, part):
    columns = HEADS * HEAD_DIM
    base_rows = jax.random.normal(jax.random.fold_in(key, 31), (SEQ, columns), jnp.float32)
    return jnp.clip(base_rows, -6.0, 6.0).astype(jnp.bfloat16)


def draw_keys(key, part):
    columns = KV_HEADS * HEAD_DIM
    base_rows = jax.random.normal(jax.random.fold_in(key, 35), (SEQ, columns), jnp.float32)
    return jnp.clip(base_rows, -6.0, 6.0).astype(jnp.bfloat16)


def level_of(key, shape, pieces, low, high):
    gain = 1.0
    for position, blocks in pieces:
        steps = jax.random.uniform(jax.random.fold_in(jax.random.fold_in(key, 6), position), (blocks,), jnp.float32, low / len(pieces), high / len(pieces))
        gain = gain * jnp.repeat(jnp.exp(steps), shape[position] // blocks).reshape((-1,) + (1,) * (len(shape) - 1 - position))
    return gain


def normal_values(rng, dims, scale, limit, cuts=(), kind=jnp.bfloat16):
    values = jax.random.normal(rng, dims, jnp.float32) * scale
    if len(cuts) > 0:
        values = level_of(rng, dims, cuts, -0.22, 0.18) * values
    return jnp.clip(values, min=-limit, max=limit).astype(kind)


def setup_inputs(seed: int = 0) -> dict:
    arg_keys = jax.random.split(jax.random.key(seed), 6)
    return {
        "queries": draw_queries(jax.random.fold_in(arg_keys[5], 71), 0),
        "keys": draw_keys(jax.random.fold_in(arg_keys[5], 71), 0),
        "values": normal_values(arg_keys[2], (SEQ, KV_HEADS * HEAD_DIM), 1.0, 6.0, ((0, 256),)),
        "grad_out": normal_values(arg_keys[3], (SEQ, HEADS * HEAD_DIM), 1.0, 6.0, ((0, 256),)),
        "doc_ids": draw_doc_ids(jax.random.fold_in(arg_keys[5], 71), 0),
    }


masked_value = -1e+30

def reference(queries, keys, values, grad_out, doc_ids):
    inv_root = 1.0 / math.sqrt(HEAD_DIM)
    group_size = HEADS // KV_HEADS
    tile_rows = min(512, SEQ)
    key_width = MOST + tile_rows
    tile_count = SEQ // tile_rows
    q_four = queries.reshape(SEQ, KV_HEADS, group_size, HEAD_DIM)
    g_four = grad_out.reshape(SEQ, KV_HEADS, group_size, HEAD_DIM)
    k_padded = jnp.concatenate([jnp.zeros((MOST, KV_HEADS * HEAD_DIM), keys.dtype), keys], 0).reshape(MOST + SEQ, KV_HEADS, HEAD_DIM)
    v_padded = jnp.concatenate([jnp.zeros((MOST, KV_HEADS * HEAD_DIM), values.dtype), values], 0).reshape(MOST + SEQ, KV_HEADS, HEAD_DIM)
    doc_padded = jnp.concatenate([jnp.full((MOST,), -1, jnp.int32), doc_ids.astype(jnp.int32)], 0)

    def one_tile(running, step_index):
        dk_acc, dv_acc = running
        tile_start = (step_index * tile_rows).astype(jnp.int32)
        q_tile = lax.dynamic_slice_in_dim(q_four, tile_start, tile_rows, 0).astype(jnp.float32)
        g_tile = lax.dynamic_slice_in_dim(g_four, tile_start, tile_rows, 0).astype(jnp.float32)
        k_tile = lax.dynamic_slice_in_dim(k_padded, tile_start, key_width, 0).astype(jnp.float32)
        v_tile = lax.dynamic_slice_in_dim(v_padded, tile_start, key_width, 0).astype(jnp.float32)
        q_docs = lax.dynamic_slice_in_dim(doc_ids.astype(jnp.int32), tile_start, tile_rows, 0)
        k_docs = lax.dynamic_slice_in_dim(doc_padded, tile_start, key_width, 0)
        q_place = jnp.arange(tile_rows, dtype=jnp.int32)
        k_place = jnp.arange(key_width, dtype=jnp.int32) - MOST
        allowed = (k_place[None, :] <= q_place[:, None]) & (k_docs[None, :] == q_docs[:, None])
        scores = jnp.einsum('qgrd,kgd->grqk', q_tile, k_tile) * inv_root
        scores = jnp.where(allowed, scores, masked_value)
        row_max = lax.optimization_barrier(jnp.max(scores, axis=-1, keepdims=True))
        raised = jnp.exp(scores - row_max)
        weights = raised / lax.optimization_barrier(jnp.sum(raised, axis=-1, keepdims=True))
        weights_f = lax.optimization_barrier(weights.astype(jnp.bfloat16)).astype(jnp.float32)
        attended = jnp.einsum('grqk,kgd->qgrd', weights_f, v_tile)
        row_dot = jnp.transpose(lax.optimization_barrier(jnp.sum(g_tile * attended, axis=-1)), (1, 2, 0))
        dweights = jnp.einsum('qgrd,kgd->grqk', g_tile, v_tile)
        d_scores = weights * (dweights - row_dot[..., None])
        d_scores = lax.optimization_barrier(d_scores.astype(jnp.bfloat16)).astype(jnp.float32)
        dq_tile = (jnp.einsum('grqk,kgd->qgrd', d_scores, k_tile) * inv_root).astype(jnp.bfloat16)
        dk_tile = jnp.einsum('grqk,qgrd->kgd', d_scores, q_tile) * inv_root
        dv_tile = jnp.einsum('grqk,qgrd->kgd', weights_f, g_tile)
        dk_acc = lax.dynamic_update_slice_in_dim(dk_acc, lax.dynamic_slice_in_dim(dk_acc, tile_start, key_width, 0) + dk_tile, tile_start, 0)
        dv_acc = lax.dynamic_update_slice_in_dim(dv_acc, lax.dynamic_slice_in_dim(dv_acc, tile_start, key_width, 0) + dv_tile, tile_start, 0)
        return ((dk_acc, dv_acc), dq_tile)
    zero_acc = jnp.zeros((MOST + SEQ, KV_HEADS, HEAD_DIM), jnp.float32)
    (dk_acc, dv_acc), dq_tiles = lax.scan(one_tile, (zero_acc, zero_acc), jnp.arange(tile_count, dtype=jnp.int32))
    grad_queries = dq_tiles.reshape(SEQ, HEADS * HEAD_DIM)
    grad_keys = dk_acc[MOST:].reshape(SEQ, KV_HEADS * HEAD_DIM).astype(jnp.bfloat16)
    grad_values = dv_acc[MOST:].reshape(SEQ, KV_HEADS * HEAD_DIM).astype(jnp.bfloat16)
    return (grad_queries, grad_keys, grad_values)
```

```python
import functools
import math

import jax
import jax.numpy as jnp
from jax import lax
from jax.experimental import pallas as pl
from jax.experimental.pallas import tpu as pltpu
from jax.sharding import PartitionSpec as P

DIM = 128
REACH = 8
SLOTS = REACH + 1
MESH = pl.DeviceIdType.MESH
MASKED = -1e30
F32 = jnp.float32
BF16 = jnp.bfloat16


def contract(a, b, dims):
    return lax.dot_general(a, b, (dims, ((), ())), preferred_element_type=F32)


def kernel(
    blks, swaps, kv_heads, share,
    q_hbm, g_hbm, k_hbm, v_hbm, docs,
    dq_out, dk_out, dv_out,
    qv, gv, kvb, kt, bias, pf, dpf, pt, dst, acc, outbox, inbox,
    load_sem, own_sem, get_send, get_recv, put_send, put_recv,
):
    total = blks * swaps
    me = lax.axis_index("blk") * swaps + lax.axis_index("swap")
    inv_root = 1.0 / math.sqrt(DIM)
    to_exp2 = inv_root * math.log2(math.e)
    tiles = share // 2

    def device(offset):
        other = lax.rem(me + (offset + total), total)
        return {"blk": lax.div(other, swaps), "swap": lax.rem(other, swaps)}

    def own_copy(group, part):
        source = (k_hbm, v_hbm)[part]
        return pltpu.make_async_copy(
            source.at[:, pl.ds(group * DIM, DIM)],
            kvb.at[group, 0, :, pl.ds(part * DIM, DIM)],
            own_sem.at[group, part],
        )

    def get_copy(group, source, target, offset, lane):
        return pltpu.make_async_remote_copy(
            src_ref=kvb.at[group, source],
            dst_ref=kvb.at[group, target],
            send_sem=get_send.at[group, lane],
            recv_sem=get_recv.at[group, target],
            device_id=device(offset),
            device_id_type=MESH,
        )

    def put_copy(group, source, target, offset):
        return pltpu.make_async_remote_copy(
            src_ref=outbox.at[group, source],
            dst_ref=inbox.at[group, target],
            send_sem=put_send.at[group, source],
            recv_sem=put_recv.at[group, target],
            device_id=device(offset),
            device_id_type=MESH,
        )

    def get_wait(group, slot):
        get_copy(group, slot, slot, 1, 0).wait_recv()

    def put_wait(group, slot):
        put_copy(group, 1, slot, 1).wait_recv()

    def relay(group, level):
        near, far = level, SLOTS - level
        get_wait(group, near)
        get_copy(group, near, near + 1, 1, near).start()
        get_wait(group, far)
        get_copy(group, far, far - 1, -1, far - 1).start()

    def ship(group, near, far, first):
        for slot in (near, far):
            value = acc[group, slot]
            if not first:
                put_wait(group, slot)
                value = value + inbox[group, slot].astype(F32)
            outbox[group, slot] = value.astype(BF16)
            if slot == near:
                put_copy(group, slot, slot - 1, -1).start()
            elif slot < REACH:
                put_copy(group, slot, slot + 1, 1).start()
            else:
                put_copy(group, slot, slot + 1, -REACH).start()

    def settle(group):
        put_wait(group, 0)
        put_wait(group, SLOTS)
        value = acc[group, 0] + inbox[group, 0].astype(F32) + inbox[group, SLOTS].astype(F32)
        at = pl.multiple_of(group * DIM, DIM)
        dk_out[:, pl.ds(at, DIM)] = value[:, :DIM].astype(BF16)
        dv_out[:, pl.ds(at, DIM)] = value[:, DIM:].astype(BF16)

    q_load = pltpu.make_async_copy(q_hbm, qv, load_sem.at[0])
    g_load = pltpu.make_async_copy(g_hbm, gv, load_sem.at[1])
    for group in range(kv_heads):
        for part in range(2):
            own_copy(group, part).start()
    q_load.start()
    g_load.start()

    barrier = pltpu.get_barrier_semaphore()
    for offset in (1, -1, REACH, -REACH):
        pl.semaphore_signal(barrier, inc=1, device_id=device(offset), device_id_type=MESH)
    pl.semaphore_wait(barrier, 4)

    for group in range(kv_heads):
        for part in range(2):
            own_copy(group, part).wait()
        get_copy(group, 0, 1, 1, 0).start()
        get_copy(group, 0, REACH, REACH, REACH).start()

    q_docs = docs[pl.ds(me, 1), :].astype(F32)
    causal = lax.broadcasted_iota(jnp.int32, (DIM, DIM), 0) <= lax.broadcasted_iota(
        jnp.int32, (DIM, DIM), 1
    )
    for slot in range(SLOTS):
        row = docs[pl.ds(lax.rem(me + (total - slot), total), 1), :].astype(F32)
        row = jnp.where(me >= slot, row, -1.0)
        k_docs = jnp.transpose(jnp.broadcast_to(row, (DIM, DIM)))
        allowed = k_docs == q_docs
        if slot == 0:
            allowed = allowed & causal
        bias[slot] = jnp.where(allowed, 0.0, MASKED)
    q_load.wait()
    g_load.wait()

    for level in range(1, 4):
        relay(0, level)
        if level > 1 and kv_heads > 1:
            relay(1, level - 1)

    def stacked(ref, group, first, count):
        at = (group * share + first) * DIM
        return jnp.concatenate(
            [ref[:, pl.ds(pl.multiple_of(at + i * DIM, DIM), DIM)] for i in range(count)], 0
        )

    def tile(group, index):
        q_rows = stacked(qv, group, 2 * index, 2)
        g_rows = stacked(gv, group, 2 * index, 2)
        tops, sums, dots = [], [], []
        for slot in range(SLOTS):
            part = bias[slot]
            scores = contract(kvb[group, slot, :, :DIM], q_rows, ((1,), (1,)))
            dweights = contract(kvb[group, slot, :, DIM:], g_rows, ((1,), (1,)))
            scores = scores * to_exp2 + jnp.concatenate([part, part], 1)
            top = jnp.max(scores, 0, keepdims=True)
            raised = jnp.exp2(scores - top)
            tops.append(top)
            sums.append(jnp.sum(raised, 0, keepdims=True))
            dots.append(jnp.sum(raised * dweights, 0, keepdims=True))
            pf[slot] = raised
            dpf[slot] = dweights
        top = functools.reduce(jnp.maximum, tops)
        factors = [jnp.exp2(t - top) for t in tops]
        inverse = 1.0 / sum(f * s for f, s in zip(factors, sums))
        row_dot = sum(f * d for f, d in zip(factors, dots)) * inverse
        columns = pl.ds(index * 2 * DIM, 2 * DIM)
        for slot in range(SLOTS):
            weights = pf[slot] * (factors[slot] * inverse)
            d_scores = weights * (dpf[slot] - row_dot)
            rows = pl.ds(slot * DIM, DIM)
            pt[rows, columns] = weights.astype(BF16)
            dst[rows, columns] = d_scores.astype(BF16)
        dq = contract(kt[...], dst[:, columns], ((1,), (0,))) * inv_root
        for i in range(2):
            at = pl.multiple_of((group * share + 2 * index + i) * DIM, DIM)
            dq_out[:, pl.ds(at, DIM)] = jnp.transpose(dq[:, i * DIM : (i + 1) * DIM]).astype(BF16)

    def one_group(group, carry):
        get_wait(group, 4)
        get_wait(group, 5)
        for slot in range(SLOTS):
            kt[:, slot * DIM : (slot + 1) * DIM] = jnp.transpose(kvb[group, slot, :, :DIM])
        for index in range(tiles):
            tile(group, index)
            if index == 0:

                @pl.when(group + 2 < kv_heads)
                def _():
                    relay(group + 2, 1)

                @pl.when(group + 1 < kv_heads)
                def _():
                    relay(group + 1, 3)

                @pl.when(group >= 1)
                def _():
                    ship(group - 1, 3, 6, False)

            if index == 1:

                @pl.when(group >= 2)
                def _():
                    settle(group - 2)

            if index == 2:

                @pl.when(group + 2 < kv_heads)
                def _():
                    relay(group + 2, 2)

                @pl.when(group >= 1)
                def _():
                    ship(group - 1, 2, 7, False)

        dv = contract(pt[...], stacked(gv, group, 0, share), ((1,), (0,)))
        dk = contract(dst[...], stacked(qv, group, 0, share), ((1,), (0,))) * inv_root
        for slot in range(SLOTS):
            rows = slice(slot * DIM, (slot + 1) * DIM)
            acc[group, slot, :, :DIM] = dk[rows]
            acc[group, slot, :, DIM:] = dv[rows]
        ship(group, 4, 5, True)

        @pl.when(group >= 1)
        def _():
            ship(group - 1, 1, 8, False)

        return carry

    lax.fori_loop(0, kv_heads, one_group, 0)

    last = kv_heads - 1
    ship(last, 3, 6, False)
    ship(last, 2, 7, False)
    settle(last - 1)
    ship(last, 1, 8, False)
    settle(last)
    for group in range(kv_heads):
        for lane in (0, 1, 2, 3, 8, 7, 6, 5):
            get_copy(group, 0, 1, 1, lane).wait_send()
        for slot in range(1, SLOTS):
            put_copy(group, slot, 0, 1).wait_send()


def body(queries, keys, values, grad_out, doc_ids):
    rows = queries.shape[0]
    heads = queries.shape[1] // DIM
    kv_heads = keys.shape[1] // DIM
    share = heads // kv_heads
    blks, swaps = lax.axis_size("blk"), lax.axis_size("swap")
    docs = doc_ids.reshape(blks * swaps, rows)
    hbm = pl.BlockSpec(memory_space=pl.ANY)
    vmem = pl.BlockSpec(memory_space=pltpu.VMEM)
    width = share * DIM
    return pl.pallas_call(
        functools.partial(kernel, blks, swaps, kv_heads, share),
        name="attention_backward",
        out_shape=(
            jax.ShapeDtypeStruct(queries.shape, BF16),
            jax.ShapeDtypeStruct(keys.shape, BF16),
            jax.ShapeDtypeStruct(values.shape, BF16),
        ),
        in_specs=[hbm, hbm, hbm, hbm, vmem],
        out_specs=(vmem, vmem, vmem),
        scratch_shapes=[
            pltpu.VMEM(queries.shape, BF16),
            pltpu.VMEM(queries.shape, BF16),
            pltpu.VMEM((kv_heads, SLOTS, DIM, 2 * DIM), BF16),
            pltpu.VMEM((DIM, SLOTS * DIM), BF16),
            pltpu.VMEM((SLOTS, DIM, DIM), F32),
            pltpu.VMEM((SLOTS, DIM, 2 * DIM), F32),
            pltpu.VMEM((SLOTS, DIM, 2 * DIM), F32),
            pltpu.VMEM((SLOTS * DIM, width), BF16),
            pltpu.VMEM((SLOTS * DIM, width), BF16),
            pltpu.VMEM((kv_heads, SLOTS, DIM, 2 * DIM), F32),
            pltpu.VMEM((kv_heads, SLOTS, DIM, 2 * DIM), BF16),
            pltpu.VMEM((kv_heads, SLOTS + 1, DIM, 2 * DIM), BF16),
            pltpu.SemaphoreType.DMA((2,)),
            pltpu.SemaphoreType.DMA((kv_heads, 2)),
            pltpu.SemaphoreType.DMA((kv_heads, SLOTS)),
            pltpu.SemaphoreType.DMA((kv_heads, SLOTS)),
            pltpu.SemaphoreType.DMA((kv_heads, SLOTS)),
            pltpu.SemaphoreType.DMA((kv_heads, SLOTS + 1)),
        ],
        compiler_params=pltpu.CompilerParams(
            collective_id=0, has_side_effects=True, vmem_limit_bytes=60 * 1024 * 1024
        ),
    )(queries, grad_out, keys, values, docs)


def solution(mesh):
    spec = P(("blk", "swap"), None)
    return jax.shard_map(
        body,
        mesh=mesh,
        in_specs=(spec, spec, spec, spec, P()),
        out_specs=(spec, spec, spec),
        check_vma=False,
    )
```

```python
import functools
import math

import jax
import jax.numpy as jnp
from jax import lax
from jax.experimental import pallas as pl
from jax.experimental.pallas import tpu as pltpu
from jax.sharding import PartitionSpec as P

DIM = 128
REACH = 8
SLOTS = REACH + 1
MESH = pl.DeviceIdType.MESH
MASKED = -1e30
F32 = jnp.float32
BF16 = jnp.bfloat16


def contract(a, b, dims):
    return lax.dot_general(a, b, (dims, ((), ())), preferred_element_type=F32)


def tree(cross):
    parents = {}
    for z in range(REACH):
        for slot in range(1, SLOTS):
            ours, block = (True, z - slot) if slot <= z else (False, z - slot + REACH)
            rank = block if ours else REACH - 1 - block
            far = (z if ours else REACH - 1 - z) > REACH // 2 + rank
            if slot == REACH:
                kind = "jump"
            elif far and rank == 0:
                kind = ("over_down" if z == REACH - 1 else "down") if ours else ("over_up" if z == 0 else "up")
            elif far and rank <= cross:
                kind = ("cross_down" if z == REACH - 1 else "down") if ours else ("cross_up" if z == 0 else "up")
            else:
                kind = "up" if ours else "down"
            parents[slot, z] = kind
    return parents


STEP = {"up": 1, "down": -1, "over_up": 1 - REACH, "over_down": REACH - 1, "jump": REACH, "cross_up": 1, "cross_down": -1}
SHIFT = {**STEP, "over_up": 1 - REACH, "over_down": REACH - 1}
CROSS = 2
LAG = 1
SHIP_AT = (2,)
PARENTS = tree(CROSS)


def depth_of(slot, z):
    if slot == 0:
        return 0
    kind = PARENTS[slot, z]
    place = (z - STEP[kind]) % REACH
    return 1 + depth_of(slot - SHIFT[kind], place)


DEPTH = {key: depth_of(*key) for key in PARENTS}
LAST = max(DEPTH.values())
EDGES = sorted({(slot - SHIFT[kind], kind) for (slot, z), kind in PARENTS.items()})


def senders(edge):
    slot, kind = edge
    child = slot + SHIFT[kind]
    return frozenset((z - STEP[kind]) % REACH for z in range(REACH) if PARENTS.get((child, z)) == kind)


def kernel(
    blks, swaps, kv_heads, share,
    q_hbm, g_hbm, k_hbm, v_hbm, docs,
    dq_out, dk_out, dv_out,
    qv, gv, kvb, kt, bias, pf, dpf, pt, dst, acc, outbox, inbox,
    load_sem, own_sem, get_send, get_recv, put_send, put_recv,
):
    total = blks * swaps
    me = lax.axis_index("blk") * swaps + lax.axis_index("swap")
    place = lax.rem(me, REACH)
    inv_root = 1.0 / math.sqrt(DIM)
    to_exp2 = inv_root * math.log2(math.e)
    tiles = share // 2

    def among(places, run):
        places = sorted(places)
        if len(places) == REACH:
            run()
        elif places:
            tests = []
            start = previous = places[0]
            for z in places[1:] + [None]:
                if z is None or z != previous + 1:
                    if start == previous:
                        tests.append(place == start)
                    elif start == 0:
                        tests.append(place <= previous)
                    elif previous == REACH - 1:
                        tests.append(place >= start)
                    else:
                        tests.append((place >= start) & (place <= previous))
                    start = z
                previous = z
            pl.when(functools.reduce(jnp.logical_or, tests))(run)

    def device(offset):
        other = lax.rem(me + (offset + total), total)
        return {"blk": lax.div(other, swaps), "swap": lax.rem(other, swaps)}

    def own_copy(group, part):
        source = (k_hbm, v_hbm)[part]
        return pltpu.make_async_copy(
            source.at[:, pl.ds(group * DIM, DIM)],
            kvb.at[group, 0, :, pl.ds(part * DIM, DIM)],
            own_sem.at[group, part],
        )

    def get_copy(group, edge):
        slot, kind = EDGES[edge]
        child = slot + SHIFT[kind]
        return pltpu.make_async_remote_copy(
            src_ref=kvb.at[group, slot],
            dst_ref=kvb.at[group, child],
            send_sem=get_send.at[group, edge],
            recv_sem=get_recv.at[group, child],
            device_id=device(STEP[kind]),
            device_id_type=MESH,
        )

    def put_copy(group, edge):
        slot, kind = EDGES[edge]
        child = slot + SHIFT[kind]
        return pltpu.make_async_remote_copy(
            src_ref=outbox.at[group, child],
            dst_ref=inbox.at[group, edge],
            send_sem=put_send.at[group, child],
            recv_sem=put_recv.at[group, edge],
            device_id=device(-STEP[kind]),
            device_id_type=MESH,
        )

    def receivers(edge):
        slot, kind = EDGES[edge]
        return frozenset((z + STEP[kind]) % REACH for z in senders(EDGES[edge]))

    def forward(group, slot, places):
        for edge, (source, _) in enumerate(EDGES):
            if source == slot:
                among(senders(EDGES[edge]) & places, lambda edge=edge: get_copy(group, edge).start())

    def relay(group, depth):
        for slot in range(1, SLOTS):
            places = frozenset(z for z in range(REACH) if DEPTH[slot, z] == depth)

            def run(slot=slot, places=places):
                edge = next(e for e, (s, kind) in enumerate(EDGES) if s + SHIFT[kind] == slot)
                get_copy(group, edge).wait_recv()
                forward(group, slot, places)

            among(places, run)

    def gathered(group, slot, places):
        for edge, (source, _) in enumerate(EDGES):
            if source == slot:

                def run(edge=edge):
                    put_copy(group, edge).wait_recv()
                    acc[group, slot] += inbox[group, edge].astype(F32)

                among(senders(EDGES[edge]) & places, run)

    def ship(group, depth):
        for slot in range(1, SLOTS):
            places = frozenset(z for z in range(REACH) if DEPTH[slot, z] == depth)

            def run(slot=slot, places=places):
                gathered(group, slot, places)
                outbox[group, slot] = acc[group, slot].astype(BF16)
                for edge, (source, kind) in enumerate(EDGES):
                    if source + SHIFT[kind] == slot:
                        among(receivers(edge) & places, lambda edge=edge: put_copy(group, edge).start())

            among(places, run)

    def settle(group):
        gathered(group, 0, frozenset(range(REACH)))
        value = acc[group, 0]
        at = pl.multiple_of(group * DIM, DIM)
        dk_out[:, pl.ds(at, DIM)] = value[:, :DIM].astype(BF16)
        dv_out[:, pl.ds(at, DIM)] = value[:, DIM:].astype(BF16)

    q_load = pltpu.make_async_copy(q_hbm, qv, load_sem.at[0])
    g_load = pltpu.make_async_copy(g_hbm, gv, load_sem.at[1])
    for group in range(kv_heads):
        for part in range(2):
            own_copy(group, part).start()
    q_load.start()
    g_load.start()

    barrier = pltpu.get_barrier_semaphore()
    offsets = (1, -1, REACH, -REACH, REACH - 1, 1 - REACH)
    for offset in offsets:
        pl.semaphore_signal(barrier, inc=1, device_id=device(offset), device_id_type=MESH)
    pl.semaphore_wait(barrier, len(offsets))

    for group in range(kv_heads):
        for part in range(2):
            own_copy(group, part).wait()
        forward(group, 0, frozenset(range(REACH)))

    q_docs = docs[pl.ds(me, 1), :].astype(F32)
    causal = lax.broadcasted_iota(jnp.int32, (DIM, DIM), 0) <= lax.broadcasted_iota(
        jnp.int32, (DIM, DIM), 1
    )
    for slot in range(SLOTS):
        row = docs[pl.ds(lax.rem(me + (total - slot), total), 1), :].astype(F32)
        row = jnp.where(me >= slot, row, -1.0)
        k_docs = jnp.transpose(jnp.broadcast_to(row, (DIM, DIM)))
        allowed = k_docs == q_docs
        if slot == 0:
            allowed = allowed & causal
        bias[slot] = jnp.where(allowed, 0.0, MASKED)
    q_load.wait()
    g_load.wait()

    for depth in range(1, LAST + 1):
        for group in range(kv_heads):
            if depth - LAG * group >= 1:
                relay(group, depth - LAG * group)

    def stacked(ref, group, first, count):
        at = (group * share + first) * DIM
        return jnp.concatenate(
            [ref[:, pl.ds(pl.multiple_of(at + i * DIM, DIM), DIM)] for i in range(count)], 0
        )

    def tile(group, index):
        q_rows = stacked(qv, group, 2 * index, 2)
        g_rows = stacked(gv, group, 2 * index, 2)
        tops, sums, dots = [], [], []
        for slot in range(SLOTS):
            part = bias[slot]
            scores = contract(kvb[group, slot, :, :DIM], q_rows, ((1,), (1,)))
            dweights = contract(kvb[group, slot, :, DIM:], g_rows, ((1,), (1,)))
            scores = scores * to_exp2 + jnp.concatenate([part, part], 1)
            top = jnp.max(scores, 0, keepdims=True)
            raised = jnp.exp2(scores - top)
            tops.append(top)
            sums.append(jnp.sum(raised, 0, keepdims=True))
            dots.append(jnp.sum(raised * dweights, 0, keepdims=True))
            pf[slot] = raised
            dpf[slot] = dweights
        top = functools.reduce(jnp.maximum, tops)
        factors = [jnp.exp2(t - top) for t in tops]
        inverse = 1.0 / sum(f * s for f, s in zip(factors, sums))
        row_dot = sum(f * d for f, d in zip(factors, dots)) * inverse
        columns = pl.ds(index * 2 * DIM, 2 * DIM)
        for slot in range(SLOTS):
            weights = pf[slot] * (factors[slot] * inverse)
            d_scores = weights * (dpf[slot] - row_dot)
            rows = pl.ds(slot * DIM, DIM)
            pt[rows, columns] = weights.astype(BF16)
            dst[rows, columns] = d_scores.astype(BF16)
        dq = contract(kt[...], dst[:, columns], ((1,), (0,))) * inv_root
        for i in range(2):
            at = pl.multiple_of((group * share + 2 * index + i) * DIM, DIM)
            dq_out[:, pl.ds(at, DIM)] = jnp.transpose(dq[:, i * DIM : (i + 1) * DIM]).astype(BF16)

    def one_group(group, carry):
        for slot in range(SLOTS):
            kt[:, slot * DIM : (slot + 1) * DIM] = jnp.transpose(kvb[group, slot, :, :DIM])
        for index in range(tiles):
            tile(group, index)
            if index % 2 == 0 and index // 2 < LAG:
                for ahead in range(1, kv_heads):
                    depth = LAST - LAG * ahead + index // 2 + 1
                    if depth >= 1:
                        pl.when(group + ahead < kv_heads)(
                            lambda ahead=ahead, depth=depth: relay(group + ahead, depth)
                        )
            if index in SHIP_AT:
                for behind in range(1, kv_heads):
                    depth = LAST - (len(SHIP_AT) * (behind - 1) + SHIP_AT.index(index)) - 1
                    if depth >= 1:
                        pl.when(group >= behind)(
                            lambda behind=behind, depth=depth: ship(group - behind, depth)
                        )
                    elif depth == 0:
                        pl.when(group >= behind)(lambda behind=behind: settle(group - behind))

        dv = contract(pt[...], stacked(gv, group, 0, share), ((1,), (0,)))
        dk = contract(dst[...], stacked(qv, group, 0, share), ((1,), (0,))) * inv_root
        for slot in range(SLOTS):
            rows = slice(slot * DIM, (slot + 1) * DIM)
            acc[group, slot, :, :DIM] = dk[rows]
            acc[group, slot, :, DIM:] = dv[rows]
        ship(group, LAST)
        return carry

    lax.fori_loop(0, kv_heads, one_group, 0)

    for index in range(LAST):
        for group in range(kv_heads):
            depth = LAST - 1 - (len(SHIP_AT) * (kv_heads - 1 - group) + index)
            if depth >= 1:
                ship(group, depth)
            elif depth == 0:
                settle(group)
    for group in range(kv_heads):
        for edge in range(len(EDGES)):
            among(senders(EDGES[edge]), lambda group=group, edge=edge: get_copy(group, edge).wait_send())
            among(receivers(edge), lambda group=group, edge=edge: put_copy(group, edge).wait_send())


def body(queries, keys, values, grad_out, doc_ids):
    rows = queries.shape[0]
    heads = queries.shape[1] // DIM
    kv_heads = keys.shape[1] // DIM
    share = heads // kv_heads
    blks, swaps = lax.axis_size("blk"), lax.axis_size("swap")
    docs = doc_ids.reshape(blks * swaps, rows)
    hbm = pl.BlockSpec(memory_space=pl.ANY)
    vmem = pl.BlockSpec(memory_space=pltpu.VMEM)
    width = share * DIM
    return pl.pallas_call(
        functools.partial(kernel, blks, swaps, kv_heads, share),
        name="attention_backward",
        out_shape=(
            jax.ShapeDtypeStruct(queries.shape, BF16),
            jax.ShapeDtypeStruct(keys.shape, BF16),
            jax.ShapeDtypeStruct(values.shape, BF16),
        ),
        in_specs=[hbm, hbm, hbm, hbm, vmem],
        out_specs=(vmem, vmem, vmem),
        scratch_shapes=[
            pltpu.VMEM(queries.shape, BF16),
            pltpu.VMEM(queries.shape, BF16),
            pltpu.VMEM((kv_heads, SLOTS, DIM, 2 * DIM), BF16),
            pltpu.VMEM((DIM, SLOTS * DIM), BF16),
            pltpu.VMEM((SLOTS, DIM, DIM), F32),
            pltpu.VMEM((SLOTS, DIM, 2 * DIM), F32),
            pltpu.VMEM((SLOTS, DIM, 2 * DIM), F32),
            pltpu.VMEM((SLOTS * DIM, width), BF16),
            pltpu.VMEM((SLOTS * DIM, width), BF16),
            pltpu.VMEM((kv_heads, SLOTS, DIM, 2 * DIM), F32),
            pltpu.VMEM((kv_heads, SLOTS, DIM, 2 * DIM), BF16),
            pltpu.VMEM((kv_heads, len(EDGES), DIM, 2 * DIM), BF16),
            pltpu.SemaphoreType.DMA((2,)),
            pltpu.SemaphoreType.DMA((kv_heads, 2)),
            pltpu.SemaphoreType.DMA((kv_heads, len(EDGES))),
            pltpu.SemaphoreType.DMA((kv_heads, SLOTS)),
            pltpu.SemaphoreType.DMA((kv_heads, SLOTS)),
            pltpu.SemaphoreType.DMA((kv_heads, len(EDGES))),
        ],
        compiler_params=pltpu.CompilerParams(
            collective_id=0, has_side_effects=True, vmem_limit_bytes=60 * 1024 * 1024
        ),
    )(queries, grad_out, keys, values, docs)


def solution(mesh):
    spec = P(("blk", "swap"), None)
    return jax.shard_map(
        body,
        mesh=mesh,
        in_specs=(spec, spec, spec, spec, P()),
        out_specs=(spec, spec, spec),
        check_vma=False,
    )
```

```python
import functools
import math

import jax
import jax.numpy as jnp
from jax import lax
from jax.experimental import pallas as pl
from jax.experimental.pallas import tpu as pltpu
from jax.sharding import PartitionSpec as P

DIM = 128
REACH = 8
SLOTS = REACH + 1
MESH = pl.DeviceIdType.MESH
MASKED = -1e30
F32 = jnp.float32
BF16 = jnp.bfloat16


def contract(a, b, dims):
    return lax.dot_general(a, b, (dims, ((), ())), preferred_element_type=F32)


def tree(cross):
    parents = {}
    for z in range(REACH):
        for slot in range(1, SLOTS):
            ours, block = (True, z - slot) if slot <= z else (False, z - slot + REACH)
            rank = block if ours else REACH - 1 - block
            far = (z if ours else REACH - 1 - z) > REACH // 2 + rank
            if slot == REACH:
                kind = "jump"
            elif far and rank == 0:
                kind = ("over_down" if z == REACH - 1 else "down") if ours else ("over_up" if z == 0 else "up")
            elif far and rank <= cross:
                kind = ("cross_down" if z == REACH - 1 else "down") if ours else ("cross_up" if z == 0 else "up")
            else:
                kind = "up" if ours else "down"
            parents[slot, z] = kind
    return parents


STEP = {"up": 1, "down": -1, "over_up": 1 - REACH, "over_down": REACH - 1, "jump": REACH, "cross_up": 1, "cross_down": -1}
SHIFT = {**STEP, "over_up": 1 - REACH, "over_down": REACH - 1}
CROSS = 2
LAG = 1
SHIP_AT = (3,)
PARENTS = tree(CROSS)


def depth_of(slot, z):
    if slot == 0:
        return 0
    kind = PARENTS[slot, z]
    place = (z - STEP[kind]) % REACH
    return 1 + depth_of(slot - SHIFT[kind], place)


DEPTH = {key: depth_of(*key) for key in PARENTS}
LAST = max(DEPTH.values())
EDGES = sorted({(slot - SHIFT[kind], kind) for (slot, z), kind in PARENTS.items()})


def senders(edge):
    slot, kind = edge
    child = slot + SHIFT[kind]
    return frozenset((z - STEP[kind]) % REACH for z in range(REACH) if PARENTS.get((child, z)) == kind)


def kernel(
    blks, swaps, kv_heads, share,
    q_hbm, g_hbm, k_hbm, v_hbm, docs,
    dq_out, dk_out, dv_out,
    qv, gv, kvb, kt, bias, pf, dpf, pt, dst, acc, outbox, inbox,
    load_sem, own_sem, get_send, get_recv, put_send, put_recv,
):
    total = blks * swaps
    me = lax.axis_index("blk") * swaps + lax.axis_index("swap")
    place = lax.rem(me, REACH)
    inv_root = 1.0 / math.sqrt(DIM)
    to_exp2 = inv_root * math.log2(math.e)
    tiles = share // 2

    def among(places, run):
        places = sorted(places)
        if len(places) == REACH:
            run()
        elif places:
            tests = []
            start = previous = places[0]
            for z in places[1:] + [None]:
                if z is None or z != previous + 1:
                    if start == previous:
                        tests.append(place == start)
                    elif start == 0:
                        tests.append(place <= previous)
                    elif previous == REACH - 1:
                        tests.append(place >= start)
                    else:
                        tests.append((place >= start) & (place <= previous))
                    start = z
                previous = z
            pl.when(functools.reduce(jnp.logical_or, tests))(run)

    def device(offset):
        other = lax.rem(me + (offset + total), total)
        return {"blk": lax.div(other, swaps), "swap": lax.rem(other, swaps)}

    def own_copy(group, part):
        source = (k_hbm, v_hbm)[part]
        return pltpu.make_async_copy(
            source.at[:, pl.ds(group * DIM, DIM)],
            kvb.at[group, 0, :, pl.ds(part * DIM, DIM)],
            own_sem.at[group, part],
        )

    def get_copy(group, edge):
        slot, kind = EDGES[edge]
        child = slot + SHIFT[kind]
        return pltpu.make_async_remote_copy(
            src_ref=kvb.at[group, slot],
            dst_ref=kvb.at[group, child],
            send_sem=get_send.at[group, edge],
            recv_sem=get_recv.at[group, child],
            device_id=device(STEP[kind]),
            device_id_type=MESH,
        )

    def put_copy(group, edge):
        slot, kind = EDGES[edge]
        child = slot + SHIFT[kind]
        return pltpu.make_async_remote_copy(
            src_ref=outbox.at[group, child],
            dst_ref=inbox.at[group, edge],
            send_sem=put_send.at[group, child],
            recv_sem=put_recv.at[group, edge],
            device_id=device(-STEP[kind]),
            device_id_type=MESH,
        )

    def receivers(edge):
        slot, kind = EDGES[edge]
        return frozenset((z + STEP[kind]) % REACH for z in senders(EDGES[edge]))

    def forward(group, slot, places):
        for edge, (source, _) in enumerate(EDGES):
            if source == slot:
                among(senders(EDGES[edge]) & places, lambda edge=edge: get_copy(group, edge).start())

    def relay(group, depth):
        for slot in range(1, SLOTS):
            places = frozenset(z for z in range(REACH) if DEPTH[slot, z] == depth)

            def run(slot=slot, places=places):
                edge = next(e for e, (s, kind) in enumerate(EDGES) if s + SHIFT[kind] == slot)
                get_copy(group, edge).wait_recv()
                forward(group, slot, places)

            among(places, run)

    def gathered(group, slot, places):
        for edge, (source, _) in enumerate(EDGES):
            if source == slot:

                def run(edge=edge):
                    put_copy(group, edge).wait_recv()
                    acc[group, slot] += inbox[group, edge].astype(F32)

                among(senders(EDGES[edge]) & places, run)

    def ship(group, depth):
        for slot in range(1, SLOTS):
            places = frozenset(z for z in range(REACH) if DEPTH[slot, z] == depth)

            def run(slot=slot, places=places):
                gathered(group, slot, places)
                outbox[group, slot] = acc[group, slot].astype(BF16)
                for edge, (source, kind) in enumerate(EDGES):
                    if source + SHIFT[kind] == slot:
                        among(receivers(edge) & places, lambda edge=edge: put_copy(group, edge).start())

            among(places, run)

    def settle(group):
        gathered(group, 0, frozenset(range(REACH)))
        value = acc[group, 0]
        at = pl.multiple_of(group * DIM, DIM)
        dk_out[:, pl.ds(at, DIM)] = value[:, :DIM].astype(BF16)
        dv_out[:, pl.ds(at, DIM)] = value[:, DIM:].astype(BF16)

    q_load = pltpu.make_async_copy(q_hbm, qv, load_sem.at[0])
    g_load = pltpu.make_async_copy(g_hbm, gv, load_sem.at[1])
    for group in range(kv_heads):
        for part in range(2):
            own_copy(group, part).start()
    q_load.start()
    g_load.start()

    barrier = pltpu.get_barrier_semaphore()
    offsets = (1, -1, REACH, -REACH, REACH - 1, 1 - REACH)
    for offset in offsets:
        pl.semaphore_signal(barrier, inc=1, device_id=device(offset), device_id_type=MESH)
    pl.semaphore_wait(barrier, len(offsets))

    for group in range(kv_heads):
        for part in range(2):
            own_copy(group, part).wait()
        forward(group, 0, frozenset(range(REACH)))

    q_docs = docs[pl.ds(me, 1), :].astype(F32)
    causal = lax.broadcasted_iota(jnp.int32, (DIM, DIM), 0) <= lax.broadcasted_iota(
        jnp.int32, (DIM, DIM), 1
    )
    for slot in range(SLOTS):
        row = docs[pl.ds(lax.rem(me + (total - slot), total), 1), :].astype(F32)
        row = jnp.where(me >= slot, row, -1.0)
        k_docs = jnp.transpose(jnp.broadcast_to(row, (DIM, DIM)))
        allowed = k_docs == q_docs
        if slot == 0:
            allowed = allowed & causal
        bias[slot] = jnp.where(allowed, 0.0, MASKED)
    q_load.wait()
    g_load.wait()

    for depth in range(1, LAST + 1):
        for group in range(kv_heads):
            if depth - LAG * group >= 1:
                relay(group, depth - LAG * group)

    def stacked(ref, group, first, count):
        at = (group * share + first) * DIM
        return jnp.concatenate(
            [ref[:, pl.ds(pl.multiple_of(at + i * DIM, DIM), DIM)] for i in range(count)], 0
        )

    def tile(group, index):
        q_rows = stacked(qv, group, 2 * index, 2)
        g_rows = stacked(gv, group, 2 * index, 2)
        tops, sums, dots = [], [], []
        for slot in range(SLOTS):
            part = bias[slot]
            scores = contract(kvb[group, slot, :, :DIM], q_rows, ((1,), (1,)))
            dweights = contract(kvb[group, slot, :, DIM:], g_rows, ((1,), (1,)))
            scores = scores * to_exp2 + jnp.concatenate([part, part], 1)
            top = jnp.max(scores, 0, keepdims=True)
            raised = jnp.exp2(scores - top)
            tops.append(top)
            sums.append(jnp.sum(raised, 0, keepdims=True))
            dots.append(jnp.sum(raised * dweights, 0, keepdims=True))
            pf[slot] = raised
            dpf[slot] = dweights
        top = functools.reduce(jnp.maximum, tops)
        factors = [jnp.exp2(t - top) for t in tops]
        inverse = 1.0 / sum(f * s for f, s in zip(factors, sums))
        row_dot = sum(f * d for f, d in zip(factors, dots)) * inverse
        columns = pl.ds(index * 2 * DIM, 2 * DIM)
        for slot in range(SLOTS):
            weights = pf[slot] * (factors[slot] * inverse)
            d_scores = weights * (dpf[slot] - row_dot)
            rows = pl.ds(slot * DIM, DIM)
            pt[rows, columns] = weights.astype(BF16)
            dst[rows, columns] = d_scores.astype(BF16)
        dq = contract(kt[...], dst[:, columns], ((1,), (0,))) * inv_root
        for i in range(2):
            at = pl.multiple_of((group * share + 2 * index + i) * DIM, DIM)
            dq_out[:, pl.ds(at, DIM)] = jnp.transpose(dq[:, i * DIM : (i + 1) * DIM]).astype(BF16)

    def one_group(group, carry):
        for slot in range(SLOTS):
            kt[:, slot * DIM : (slot + 1) * DIM] = jnp.transpose(kvb[group, slot, :, :DIM])
        for index in range(tiles):
            tile(group, index)
            if index == 1:
                for ahead in range(1, kv_heads):
                    depth = LAST - LAG * ahead + 1
                    if depth >= 1:
                        pl.when(group + ahead < kv_heads)(
                            lambda ahead=ahead, depth=depth: relay(group + ahead, depth)
                        )
            if index in SHIP_AT:
                for behind in range(1, kv_heads):
                    depth = LAST - (len(SHIP_AT) * (behind - 1) + SHIP_AT.index(index)) - 1
                    if depth >= 1:
                        pl.when(group >= behind)(
                            lambda behind=behind, depth=depth: ship(group - behind, depth)
                        )
                    elif depth == 0:
                        pl.when(group >= behind)(lambda behind=behind: settle(group - behind))

        dv = contract(pt[...], stacked(gv, group, 0, share), ((1,), (0,)))
        dk = contract(dst[...], stacked(qv, group, 0, share), ((1,), (0,))) * inv_root
        for slot in range(SLOTS):
            rows = slice(slot * DIM, (slot + 1) * DIM)
            acc[group, slot, :, :DIM] = dk[rows]
            acc[group, slot, :, DIM:] = dv[rows]
        ship(group, LAST)
        return carry

    lax.fori_loop(0, kv_heads, one_group, 0)

    for index in range(LAST):
        for group in range(kv_heads):
            depth = LAST - 1 - (len(SHIP_AT) * (kv_heads - 1 - group) + index)
            if depth >= 1:
                ship(group, depth)
            elif depth == 0:
                settle(group)
    for group in range(kv_heads):
        for edge in range(len(EDGES)):
            among(senders(EDGES[edge]), lambda group=group, edge=edge: get_copy(group, edge).wait_send())
            among(receivers(edge), lambda group=group, edge=edge: put_copy(group, edge).wait_send())


def body(queries, keys, values, grad_out, doc_ids):
    rows = queries.shape[0]
    heads = queries.shape[1] // DIM
    kv_heads = keys.shape[1] // DIM
    share = heads // kv_heads
    blks, swaps = lax.axis_size("blk"), lax.axis_size("swap")
    docs = doc_ids.reshape(blks * swaps, rows)
    hbm = pl.BlockSpec(memory_space=pl.ANY)
    vmem = pl.BlockSpec(memory_space=pltpu.VMEM)
    width = share * DIM
    return pl.pallas_call(
        functools.partial(kernel, blks, swaps, kv_heads, share),
        name="attention_backward",
        out_shape=(
            jax.ShapeDtypeStruct(queries.shape, BF16),
            jax.ShapeDtypeStruct(keys.shape, BF16),
            jax.ShapeDtypeStruct(values.shape, BF16),
        ),
        in_specs=[hbm, hbm, hbm, hbm, vmem],
        out_specs=(vmem, vmem, vmem),
        scratch_shapes=[
            pltpu.VMEM(queries.shape, BF16),
            pltpu.VMEM(queries.shape, BF16),
            pltpu.VMEM((kv_heads, SLOTS, DIM, 2 * DIM), BF16),
            pltpu.VMEM((DIM, SLOTS * DIM), BF16),
            pltpu.VMEM((SLOTS, DIM, DIM), F32),
            pltpu.VMEM((SLOTS, DIM, 2 * DIM), F32),
            pltpu.VMEM((SLOTS, DIM, 2 * DIM), F32),
            pltpu.VMEM((SLOTS * DIM, width), BF16),
            pltpu.VMEM((SLOTS * DIM, width), BF16),
            pltpu.VMEM((kv_heads, SLOTS, DIM, 2 * DIM), F32),
            pltpu.VMEM((kv_heads, SLOTS, DIM, 2 * DIM), BF16),
            pltpu.VMEM((kv_heads, len(EDGES), DIM, 2 * DIM), BF16),
            pltpu.SemaphoreType.DMA((2,)),
            pltpu.SemaphoreType.DMA((kv_heads, 2)),
            pltpu.SemaphoreType.DMA((kv_heads, len(EDGES))),
            pltpu.SemaphoreType.DMA((kv_heads, SLOTS)),
            pltpu.SemaphoreType.DMA((kv_heads, SLOTS)),
            pltpu.SemaphoreType.DMA((kv_heads, len(EDGES))),
        ],
        compiler_params=pltpu.CompilerParams(
            collective_id=0, has_side_effects=True, vmem_limit_bytes=60 * 1024 * 1024
        ),
    )(queries, grad_out, keys, values, docs)


def solution(mesh):
    spec = P(("blk", "swap"), None)
    return jax.shard_map(
        body,
        mesh=mesh,
        in_specs=(spec, spec, spec, spec, P()),
        out_specs=(spec, spec, spec),
        check_vma=False,
    )
```
